32 devices in a mesh: group: 1, tile: 8 (over z, core), dp: 4 (over y, x).
Axes of the slice: x: 2, y: 2, z: 4, core: 2. Of those that a mesh axis runs over, the one named last changes fastest.
Arguments:
- activations: bfloat16 [4, 8, 24, 24, 128], P(('group', 'dp'), 'tile'), may hold values from -6 to 6
- cotangent: bfloat16 [4, 8, 24, 24, 128], P(('group', 'dp'), 'tile'), may hold values from -1.5 to 1.5
- kernel: bfloat16 [1152, 128], P('group'), may hold values from -0.1875 to 0.1875
- turning: int32 [8], P('tile'), may hold values from 0 to 3
- orient: int32 [8, 4], P('tile'), may hold values from 0 to 7, as said below
- left_factor: float32 [1152, 1152], P(('group', 'tile')), may hold values from -0.15 to 5.15
- left_basis: float32 [1152, 1152], P(('group', 'tile'), 'dp'), may hold values from -0.026516504 to 1.0265165
- right_factor: float32 [128, 128], P('group'), may hold values from -4.26 to 49.26
- right_basis: float32 [128, 128], P('group'), may hold values from -0.079549513 to 1.0795495
- momentum: float32 [1152, 128], P(('group', 'dp')), may hold values from -1.5 to 1.5
- second_moment: float32 [1152, 128], P(('group', 'dp')), may hold values from 0.02 to 0.2
Outputs:
- output: bfloat16 [4, 8, 24, 24, 128], P(('group', 'dp'), 'tile')
- input_grad: bfloat16 [4, 8, 24, 24, 128], P(('group', 'dp'), 'tile')
- kernel_grad: float32 [1152, 128], P('group')
- left_factor_new: float32 [1152, 1152], P(('group', 'tile'))
- left_basis_new: float32 [1152, 1152], P(('group', 'tile'))
- right_factor_new: float32 [128, 128], P('group')
- right_basis_new: float32 [128, 128], P('group')
- momentum_new: float32 [1152, 128], P(('group', 'dp'))
- second_new: float32 [1152, 128], P(('group', 'dp'))
- update: float32 [1152, 128], P(('group', 'tile'))
The draws below stay inside these ranges and needn't reach their ends.
Inputs may be any that keep to these rules, and one draw needn't show every extreme that they name: 0 where edge e of tile t leaves the patch; otherwise orient[t, e] % 4 is the edge of neighbor[t, e] that heads back to t, and 4 is added where the two edges' cell orders run opposite ways.
All inputs are finite; a program needn't handle non-finite values.
Results may differ from the reference program's by a relative error of at most 0.0025.
Values may be sent and summed in bfloat16 or wider, within the bound.
A program may use at most 128 MiB of HBM per device.

```python
import math
import jax
import jax.numpy as jnp
from jax import lax

C = 128
TS = 24
FL = 1152
NTILES = 8
BATCH = 4
CELLS = 18432


def tile_turns(key):
    return jax.random.randint(jax.random.fold_in(key, 12), (NTILES,), 0, 4).astype(jnp.int32)


def draw_turning(key, part):
    return tile_turns(key)


def draw_orient(key, part):
    count = NTILES
    turning = tile_turns(key)
    tile_ids = jnp.arange(count, dtype=jnp.int32)
    row_of = tile_ids // 4
    col_of = tile_ids % 4
    edges = jnp.arange(4, dtype=jnp.int32)[None, :]
    heading = (edges + turning[:, None]) % 4
    row_step = jnp.where(heading == 0, -1, jnp.where(heading == 2, 1, 0)).astype(jnp.int32)
    col_step = jnp.where(heading == 1, 1, jnp.where(heading == 3, -1, 0)).astype(jnp.int32)
    next_row = row_of[:, None] + row_step
    next_col = col_of[:, None] + col_step
    inside = (next_row >= 0) & (next_row < count // 4) & (next_col >= 0) & (next_col < 4)
    target = jnp.clip(next_row, 0, count // 4 - 1) * 4 + jnp.clip(next_col, 0, 3)
    target_turn = turning[target]
    their_edge = (heading + 2 - target_turn) % 4
    mine_dir = (1 + edges % 2 + turning[:, None]) % 4
    their_dir = (1 + their_edge % 2 + target_turn) % 4
    flip_flag = (mine_dir != their_dir).astype(jnp.int32)
    return jnp.where(inside, their_edge + 4 * flip_flag, 0).astype(jnp.int32)


def raw_noise(key, count):
    return jax.random.truncated_normal(key, -3.0, 3.0, (count, count), jnp.float32)


def symmetric_noise(key, count):
    noise = raw_noise(jax.random.fold_in(key, 5), count)
    return (noise + noise.T) * 0.5


def draw_left_factor(key, part):
    diagonal = jax.random.uniform(jax.random.fold_in(key, 3), (FL,), jnp.float32, 3.5, 5.0)
    return symmetric_noise(key, FL) * 0.05 + jnp.diag(diagonal)


def draw_right_factor(key, part):
    diagonal = jax.random.uniform(jax.random.fold_in(key, 3), (C,), jnp.float32, 30.0, 45.0)
    return symmetric_noise(key, C) * 1.42 + jnp.diag(diagonal)


def draw_left_basis(key, part):
    noise = raw_noise(jax.random.fold_in(key, 7), FL)
    return noise * (0.3 / math.sqrt(FL)) + jnp.eye(FL, dtype=jnp.float32)


def draw_right_basis(key, part):
    noise = raw_noise(jax.random.fold_in(key, 7), C)
    return noise * (0.3 / math.sqrt(C)) + jnp.eye(C, dtype=jnp.float32)


def block_scale(key, dims, shards, smallest, high):
    loudness, own = 1.0, jax.random.fold_in(key, 6)
    for position, shards_of in shards:
        steps = jnp.exp(jax.random.uniform(jax.random.fold_in(own, position), (shards_of,), jnp.float32, smallest / len(shards), high / len(shards)))
        loudness = loudness * jnp.repeat(steps, dims[position] // shards_of).reshape([-1 if axis == position else 1 for axis in range(len(dims))])
    return loudness


def gaussian(stream_key, extent, scale, reach, shards=(), held_as=jnp.bfloat16):
    entries = scale * jax.random.normal(stream_key, extent, jnp.float32)
    if shards:
        entries = entries * block_scale(stream_key, extent, shards, -0.22, 0.18)
    return jnp.clip(entries, -reach, reach).astype(held_as)


def setup_inputs(seed: int = 0, part: int = 0) -> dict:
    arg_keys = jax.random.split(jax.random.key(seed), 12)
    part_splits = jax.random.split(jax.random.fold_in(arg_keys[11], part), 12)
    return {
        "activations": gaussian(part_splits[0], (BATCH, NTILES, TS, TS, C), 1.0, 6.0, ((0, 4), (1, 8))),
        "cotangent": gaussian(part_splits[1], (BATCH, NTILES, TS, TS, C), 0.25, 1.5, ((0, 4), (1, 8))),
        "kernel": gaussian(part_splits[2], (FL, C), FL ** -0.5, 0.1875),
        "turning": draw_turning(jax.random.fold_in(arg_keys[11], 71), part),
        "orient": draw_orient(jax.random.fold_in(arg_keys[11], 71), part),
        "left_factor": draw_left_factor(jax.random.fold_in(jax.random.fold_in(arg_keys[11], part), 71), part),
        "left_basis": draw_left_basis(jax.random.fold_in(jax.random.fold_in(arg_keys[11], part), 71), part),
        "right_factor": draw_right_factor(jax.random.fold_in(jax.random.fold_in(arg_keys[11], part), 71), part),
        "right_basis": draw_right_basis(jax.random.fold_in(jax.random.fold_in(arg_keys[11], part), 71), part),
        "momentum": gaussian(part_splits[9], (FL, C), 0.25, 1.5, ((0, 4),), jnp.float32),
        "second_moment": jnp.clip(jnp.exp(math.log(0.2) - 2.3025851 * jax.random.uniform(part_splits[10], (FL, C), jnp.float32) ** block_scale(part_splits[10], (FL, C), ((0, 4),), -0.2, 0.2)), 0.02, 0.2),
    }


highest = lax.Precision.HIGHEST

def patch_layout(turning):
    count = turning.shape[0]
    tile_ids = jnp.arange(count, dtype=jnp.int32)
    row_of = tile_ids // 4
    col_of = tile_ids % 4
    heading = (jnp.arange(4, dtype=jnp.int32)[None, :] + turning[:, None]) % 4
    row_step = jnp.where(heading == 0, -1, jnp.where(heading == 2, 1, 0)).astype(jnp.int32)
    col_step = jnp.where(heading == 1, 1, jnp.where(heading == 3, -1, 0)).astype(jnp.int32)
    next_row = row_of[:, None] + row_step
    next_col = col_of[:, None] + col_step
    inside = (next_row >= 0) & (next_row < count // 4) & (next_col >= 0) & (next_col < 4)
    target = jnp.clip(next_row, 0, count // 4 - 1) * 4 + jnp.clip(next_col, 0, 3)
    return jnp.where(inside, target, -1).astype(jnp.int32)

def edge_strips(values):
    return jnp.stack([values[..., 0, :, :], values[..., :, -1, :], values[..., -1, :, :], values[..., :, 0, :]], axis=0)

def cycle_strips(spread):
    return jnp.stack([spread[:, 0, 1:-1], spread[:, 1:-1, -1], spread[:, -1, 1:-1], spread[:, 1:-1, 0]], axis=0)

def assemble(tile_vals, borders):
    middle = jnp.concatenate([borders[3][:, :, None, :], tile_vals, borders[1][:, :, None, :]], axis=2)
    top_row = jnp.pad(borders[0], ((0, 0), (1, 1), (0, 0)))[:, None]
    bottom_row = jnp.pad(borders[2], ((0, 0), (1, 1), (0, 0)))[:, None]
    return jnp.concatenate([top_row, middle, bottom_row], axis=1)

def tap_patches(padded, side):
    pieces = [padded[:, row_off:row_off + side, col_off:col_off + side, :] for row_off in range(3) for col_off in range(3)]
    joined = jnp.concatenate(pieces, axis=-1)
    return joined.reshape(-1, joined.shape[-1])

def spread_back(flat_grads, kernel, sample_count, side):
    channels = kernel.shape[1]
    summed = jnp.zeros((sample_count, side + 2, side + 2, channels), jnp.float32)
    for tap_index in range(9):
        row_off, col_off = divmod(tap_index, 3)
        weight_tap = kernel[tap_index * channels:(tap_index + 1) * channels]
        contrib = lax.dot_general(flat_grads.astype(jnp.float32), weight_tap.astype(jnp.float32), (((1,), (1,)), ((), ())), preferred_element_type=jnp.float32)
        contrib = contrib.reshape(sample_count, side, side, channels)
        summed = summed + jnp.pad(contrib, ((0, 0), (row_off, 2 - row_off), (col_off, 2 - col_off), (0, 0)))
    return summed

def absorb_rims(interior, incoming):
    result = interior.at[..., 0, :, :].add(incoming[0])
    result = result.at[..., :, -1, :].add(incoming[1])
    result = result.at[..., -1, :, :].add(incoming[2])
    return result.at[..., :, 0, :].add(incoming[3])

def route(strips, source, facing, flipped, usable):
    picked = strips[source, facing]
    picked = jnp.where(flipped[:, :, None, None, None], picked[:, :, :, ::-1, :], picked)
    return jnp.where(usable[:, :, None, None, None], picked, jnp.zeros_like(picked))

def orthonormal(power):
    gram = jnp.dot(power.T, power, precision=highest)
    lower = jnp.linalg.cholesky(gram)
    return lax.linalg.triangular_solve(lower, power.T, left_side=True, lower=True).T

def reference(activations, cotangent, kernel, turning, orient, left_factor, left_basis, right_factor, right_basis, momentum, second_moment):
    neighbor = patch_layout(turning)
    usable = neighbor >= 0
    source = jnp.where(usable, neighbor, 0).astype(jnp.int32)
    facing = (orient % 4).astype(jnp.int32)
    flipped = orient >= 4
    by_tile = jnp.swapaxes(activations, 0, 1)
    grads_tile = jnp.swapaxes(cotangent, 0, 1)
    strips = jnp.moveaxis(edge_strips(by_tile), 0, 1)
    borders = route(strips, source, facing, flipped, usable)

    def one_tile(inputs):
        tile_vals, tile_grads, tile_borders = inputs
        padded = assemble(tile_vals, tile_borders)
        columns = tap_patches(padded, TS)
        flat_grads = tile_grads.reshape(-1, C)
        result = jnp.dot(columns.astype(jnp.float32), kernel.astype(jnp.float32), preferred_element_type=jnp.float32).astype(jnp.bfloat16).reshape(tile_vals.shape)
        spread = spread_back(flat_grads, kernel, tile_vals.shape[0], TS)
        rim_cells = cycle_strips(spread).astype(jnp.bfloat16)
        interior = spread[:, 1:-1, 1:-1]
        partial_grad = lax.dot_general(columns.astype(jnp.float32), flat_grads.astype(jnp.float32), (((0,), (0,)), ((), ())), preferred_element_type=jnp.float32)
        return (result, interior, rim_cells, partial_grad)
    outputs, interiors, rims, partials = lax.map(one_tile, (by_tile, grads_tile, borders))
    incoming = route(rims, source, facing, flipped, usable).astype(jnp.float32)
    input_grad = absorb_rims(interiors, jnp.moveaxis(incoming, 1, 0)).astype(jnp.bfloat16)
    grad = lax.optimization_barrier(jnp.sum(partials, axis=0)) * (1.0 / math.sqrt(CELLS))
    left_new = 0.95 * left_factor + 0.05 * jnp.dot(grad, grad.T, precision=highest)
    right_new = 0.95 * right_factor + 0.05 * jnp.dot(grad.T, grad, precision=highest)
    basis_new = orthonormal(jnp.dot(left_new, left_basis, precision=highest))
    right_basis_new = orthonormal(jnp.dot(right_new, right_basis, precision=highest))
    back = jnp.dot(left_basis, momentum, precision=highest)
    right_turn = jnp.dot(right_basis.T, right_basis_new, precision=highest)
    rotated = jnp.dot(jnp.dot(basis_new.T, back, precision=highest), right_turn, precision=highest)
    projected = jnp.dot(jnp.dot(basis_new.T, grad, precision=highest), right_basis_new, precision=highest)
    momentum_new = 0.9 * rotated + 0.1 * projected
    second_new = 0.95 * second_moment + 0.05 * projected * projected
    normalized = momentum_new / (jnp.sqrt(second_new) + 1e-08)
    update = jnp.dot(jnp.dot(basis_new, normalized, precision=highest), right_basis_new.T, precision=highest)
    return (jnp.swapaxes(outputs, 0, 1), jnp.swapaxes(input_grad, 0, 1), grad, left_new, basis_new, right_new, right_basis_new, momentum_new, second_new, update)
```

```python
import math

import jax
import jax.numpy as jnp
from jax import lax
from jax.experimental import pallas as pl
from jax.experimental.pallas import tpu as pltpu
from jax.sharding import PartitionSpec as P

highest = lax.Precision.HIGHEST
epsilon = 1e-08


def edge_strips(values):
    return jnp.stack(
        [values[..., 0, :, :], values[..., :, -1, :], values[..., -1, :, :], values[..., :, 0, :]],
        axis=0,
    )


def cycle_strips(spread):
    return jnp.stack(
        [spread[:, 0, 1:-1], spread[:, 1:-1, -1], spread[:, -1, 1:-1], spread[:, 1:-1, 0]], axis=0
    )


def assemble(tile_vals, borders):
    middle = jnp.concatenate(
        [borders[3][:, :, None, :], tile_vals, borders[1][:, :, None, :]], axis=2
    )
    top_row = jnp.pad(borders[0], ((0, 0), (1, 1), (0, 0)))[:, None]
    bottom_row = jnp.pad(borders[2], ((0, 0), (1, 1), (0, 0)))[:, None]
    return jnp.concatenate([top_row, middle, bottom_row], axis=1)


def tap_patches(padded, side):
    pieces = [
        padded[:, row_off : row_off + side, col_off : col_off + side, :]
        for row_off in range(3)
        for col_off in range(3)
    ]
    joined = jnp.concatenate(pieces, axis=-1)
    return joined.reshape(-1, joined.shape[-1])


def spread_back(flat_grads, kernel, sample_count, side):
    channels = kernel.shape[1]
    summed = jnp.zeros((sample_count, side + 2, side + 2, channels), jnp.float32)
    for tap_index in range(9):
        row_off, col_off = divmod(tap_index, 3)
        weight_tap = kernel[tap_index * channels : (tap_index + 1) * channels]
        contrib = lax.dot_general(
            flat_grads, weight_tap, (((1,), (1,)), ((), ())), preferred_element_type=jnp.float32
        )
        contrib = contrib.reshape(sample_count, side, side, channels)
        summed = summed + jnp.pad(
            contrib, ((0, 0), (row_off, 2 - row_off), (col_off, 2 - col_off), (0, 0))
        )
    return summed


def absorb_rims(interior, incoming):
    result = interior.at[..., 0, :, :].add(incoming[0])
    result = result.at[..., :, -1, :].add(incoming[1])
    result = result.at[..., -1, :, :].add(incoming[2])
    return result.at[..., :, 0, :].add(incoming[3])


def flip_edges(strips, flipped):
    return jnp.where(flipped[:, None, None, None], strips[:, :, ::-1, :], strips)


def pick_gathered(everything, near_tiles, facing, flipped, usable):
    flat = everything.reshape(everything.shape[0] * 4, -1)
    wanted = jnp.where(usable, near_tiles * 4 + facing, -1)
    selector = (lax.broadcasted_iota(jnp.int32, (4, flat.shape[0]), 1) == wanted[:, None]).astype(
        jnp.bfloat16
    )
    picked = jnp.dot(selector, flat, preferred_element_type=jnp.float32).astype(jnp.bfloat16)
    return flip_edges(picked.reshape((4,) + everything.shape[2:]), flipped)


LEAF = 128
SPAN = 384


def split(value):
    high = value.astype(jnp.bfloat16)
    return high, (value - high.astype(jnp.float32)).astype(jnp.bfloat16)


def split_wide(value):
    high = lax.reduce_precision(value, 8, 7)
    return high.astype(jnp.bfloat16), (value - high).astype(jnp.bfloat16)


def dot3(left, right, dims=(((1,), (0,)), ((), ()))):
    def one(a, b):
        return lax.dot_general(a, b, dims, preferred_element_type=jnp.float32)

    return one(left[0], right[0]) + (one(left[0], right[1]) + one(left[1], right[0]))


by_rows = (((1,), (1,)), ((), ()))


def leaf_inverse(block, m_ref, s_ref):
    row = lax.broadcasted_iota(jnp.int32, (LEAF, LEAF), 0)
    col = lax.broadcasted_iota(jnp.int32, (LEAF, LEAF), 1)
    on_diag = row == col
    unit = jnp.where(on_diag, 1.0, 0.0)
    kept = jnp.where(on_diag, block, 0.0)
    across = lax.rsqrt(jnp.sum(kept, axis=0, keepdims=True))
    down = lax.rsqrt(jnp.sum(kept, axis=1, keepdims=True))
    scaled = block * across * down
    m_ref[...] = jnp.where(on_diag, down, jnp.where(row > col, -scaled * across, 0.0))
    pair = split(block)

    def more(carry):
        step, error = carry
        return (step < 12) & (error > 1e-4)

    def refine(carry):
        step, _ = carry
        guess = m_ref[...]
        guess_pair = split(guess)
        turned = dot3(guess_pair, pair)
        gap = dot3(split(turned), guess_pair, by_rows) - unit
        error = jnp.max(jnp.abs(gap))
        low = jnp.where(row > col, gap, jnp.where(on_diag, 0.5 * gap, 0.0))
        m_ref[...] = guess - dot3(split(low), guess_pair)
        return step + 1, error

    _, error = lax.while_loop(more, refine, (jnp.int32(0), jnp.float32(1.0)))

    @pl.when(jnp.logical_not(error <= 1e-4))
    def _():
        s_ref[...] = block
        m_ref[...] = unit

        def eliminate(j, carry):
            work = s_ref[...]
            line = s_ref[pl.ds(j, 1), :]
            lane = lax.broadcasted_iota(jnp.int32, (1, LEAF), 1)
            scale = lax.rsqrt(jnp.sum(jnp.where(lane == j, line, 0.0), axis=1, keepdims=True))
            column = jnp.sum(jnp.where(col == j, work, 0.0), axis=1, keepdims=True)
            side = lax.broadcasted_iota(jnp.int32, (LEAF, 1), 0)
            column = jnp.where(side > j, column * scale, 0.0)
            s_ref[...] = work - column * (line * scale)
            mine = m_ref[pl.ds(j, 1), :] * scale
            m_ref[...] = m_ref[...] - column * mine
            m_ref[pl.ds(j, 1), :] = mine
            return carry

        lax.fori_loop(0, LEAF, eliminate, 0)


def factor_kernel(
    gram_ref, side_ref, small_ref, y_ref, small_out_ref, a_ref, uh, ul, uth, utl, yh, yl, m_ref, s_ref
):
    width = gram_ref.shape[1]
    blocks = width // LEAF
    spans = width // SPAN
    leaf_inverse(small_ref[...], m_ref, s_ref)
    small_out_ref[...] = m_ref[...]
    a_ref[...] = gram_ref[...]
    y_ref[...] = side_ref[...]

    def block_step(k, carry):
        k0 = pl.multiple_of(k * LEAF, LEAF)
        leaf_inverse(a_ref[pl.ds(k0, LEAF), pl.ds(k0, LEAF)], m_ref, s_ref)
        inverse = split(m_ref[...])
        for span in range(spans):
            part = slice(span * SPAN, (span + 1) * SPAN)

            @pl.when((span + 1) * SPAN > k0 + LEAF)
            def _():
                value = dot3(inverse, split(a_ref[pl.ds(k0, LEAF), part]))
                uh[:, part], ul[:, part] = split(value)
                uth[part, :], utl[part, :] = split(value.T)

        value = dot3(inverse, split(y_ref[pl.ds(k0, LEAF), :]))
        y_ref[pl.ds(k0, LEAF), :] = value
        yh[...], yl[...] = split(value)

        def row_step(i, inner):
            i0 = pl.multiple_of(i * LEAF, LEAF)
            left = uth[pl.ds(i0, LEAF), :], utl[pl.ds(i0, LEAF), :]
            for span in range(spans):
                part = slice(span * SPAN, (span + 1) * SPAN)

                @pl.when((span + 1) * SPAN > i0)
                def _():
                    a_ref[pl.ds(i0, LEAF), part] -= dot3(left, (uh[:, part], ul[:, part]))

            y_ref[pl.ds(i0, LEAF), :] -= dot3(left, (yh[...], yl[...]))
            return inner

        lax.fori_loop(k + 1, blocks, row_step, 0)
        return carry

    lax.fori_loop(0, blocks, block_step, 0)


def factor_solve(gram, side, small):
    width, columns = side.shape
    vmem = pl.BlockSpec(memory_space=pltpu.VMEM)
    half = jnp.bfloat16
    return pl.pallas_call(
        factor_kernel,
        out_shape=(
            jax.ShapeDtypeStruct(side.shape, jnp.float32),
            jax.ShapeDtypeStruct(small.shape, jnp.float32),
        ),
        in_specs=[vmem] * 3,
        out_specs=(vmem, vmem),
        scratch_shapes=[
            pltpu.VMEM((width, width), jnp.float32),
            pltpu.VMEM((LEAF, width), half),
            pltpu.VMEM((LEAF, width), half),
            pltpu.VMEM((width, LEAF), half),
            pltpu.VMEM((width, LEAF), half),
            pltpu.VMEM((LEAF, columns), half),
            pltpu.VMEM((LEAF, columns), half),
            pltpu.VMEM((LEAF, LEAF), jnp.float32),
            pltpu.VMEM((LEAF, LEAF), jnp.float32),
        ],
        compiler_params=pltpu.CompilerParams(vmem_limit_bytes=40 * 1024 * 1024),
        name="factor_solve",
    )(gram, side, small)


high = lax.Precision.HIGH
tn = (((0,), (0,)), ((), ()))


def body(
    activations,
    cotangent,
    kernel,
    turning,
    orient,
    left_factor,
    left_basis,
    right_factor,
    right_basis,
    momentum,
    second_moment,
):
    tiles = lax.axis_size("tile")
    dp_count = lax.axis_size("dp")
    tile_index = lax.axis_index("tile")
    dp_index = lax.axis_index("dp")
    tile_vals = activations[:, 0]
    tile_grads = cotangent[:, 0]
    sample_count = tile_vals.shape[0]
    side = tile_vals.shape[1]
    channels = tile_vals.shape[-1]
    own_turn = turning[0]
    facing = orient[0] % 4
    flipped = orient[0] >= 4
    heading = (jnp.arange(4, dtype=jnp.int32) + own_turn) % 4
    row_of = tile_index // 4
    col_of = tile_index % 4
    room = jnp.stack([row_of > 0, col_of < 3, row_of < tiles // 4 - 1, col_of > 0])
    usable = (
        jnp.sum(
            jnp.where(
                heading[:, None] == jnp.arange(4, dtype=jnp.int32)[None, :], room[None, :], False
            ),
            axis=1,
        )
        > 0
    )
    offsets = jnp.array([-4, 1, 4, -1], dtype=jnp.int32)
    near_tiles = tile_index + jnp.sum(
        jnp.where(heading[:, None] == jnp.arange(4, dtype=jnp.int32)[None, :], offsets[None, :], 0),
        axis=1,
    )
    strips = edge_strips(tile_vals)
    everything = lax.all_gather(strips[None], "tile", axis=0, tiled=True)
    borders = pick_gathered(everything, near_tiles, facing, flipped, usable)
    padded = assemble(tile_vals, borders)
    columns = tap_patches(padded, side)
    flat_grads = tile_grads.reshape(-1, channels)
    partial_grad = lax.dot_general(
        columns, flat_grads, (((0,), (0,)), ((), ())), preferred_element_type=jnp.float32
    )
    summed_grad = lax.psum(partial_grad, ("tile", "dp"))
    result = jnp.dot(columns, kernel, preferred_element_type=jnp.float32).astype(jnp.bfloat16)
    result = result.reshape(activations.shape)
    spread = spread_back(flat_grads, kernel, sample_count, side)
    rim_cells = cycle_strips(spread).astype(jnp.bfloat16)
    all_rims = lax.all_gather(rim_cells[None], "tile", axis=0, tiled=True)
    incoming = pick_gathered(all_rims, near_tiles, facing, flipped, usable)
    input_grad = absorb_rims(spread[:, 1:-1, 1:-1], incoming.astype(jnp.float32)).astype(
        jnp.bfloat16
    )
    input_grad = input_grad.reshape(cotangent.shape)
    cells = dp_count * sample_count * tiles * side * side
    grad = summed_grad * (1.0 / math.sqrt(cells))
    rows_per, width = left_factor.shape
    row_start = tile_index * rows_per
    moment_rows = momentum.shape[0]
    moment_start = dp_index * moment_rows
    grad_rows = lax.dynamic_slice_in_dim(grad, row_start, rows_per, 0)
    left_new = 0.95 * left_factor + 0.05 * lax.dot_general(
        grad_rows, grad, (((1,), (1,)), ((), ())), precision=high
    )
    basis_rows = lax.all_gather(left_basis, "dp", axis=1, tiled=True)
    basis = lax.all_gather(basis_rows.astype(jnp.bfloat16), "tile", axis=0, tiled=True)
    moments = lax.all_gather(
        jnp.concatenate([momentum, second_moment], axis=1), "dp", axis=0, tiled=True
    )
    all_momentum, all_second = moments[:, :channels], moments[:, channels:]
    back_rows = jnp.dot(basis_rows, all_momentum, precision=highest)
    own_row = row_start + lax.broadcasted_iota(jnp.int32, left_factor.shape, 0)
    own_col = lax.broadcasted_iota(jnp.int32, left_factor.shape, 1)
    diagonal = jnp.sum(jnp.where(own_row == own_col, left_factor, 0.0), axis=1, keepdims=True)
    rest = jnp.broadcast_to(split_wide(diagonal)[1], (rows_per, LEAF))
    factor = lax.all_gather(
        jnp.concatenate(
            [left_factor.astype(jnp.bfloat16), *split_wide(back_rows), rest], axis=1
        ),
        "tile",
        axis=0,
        tiled=True,
    )
    back = factor[:, width : width + channels].astype(jnp.float32) + factor[
        :, width + channels : width + 2 * channels
    ].astype(jnp.float32)
    rest = factor[:, width + 2 * channels : width + 2 * channels + 1]
    factor = factor[:, :width]
    mapped = 0.95 * (
        jnp.dot(factor, basis, preferred_element_type=jnp.float32)
        + rest.astype(jnp.float32) * basis.astype(jnp.float32)
    )
    mapped_gram = lax.dot_general(mapped, mapped, tn, precision=high)
    mapped_back = lax.dot_general(mapped, back, tn, precision=high)
    crossed = sum(
        lax.dot_general(term, basis, tn, preferred_element_type=jnp.float32) for term in split_wide(grad)
    )
    mapped_grad = lax.dot_general(mapped, grad, tn, precision=high)
    grad_gram = lax.dot_general(grad, grad, tn, precision=high)
    grad_back = lax.dot_general(grad, back, tn, precision=high)
    weight = 0.05 * mapped_grad + 0.00125 * lax.dot_general(crossed, grad_gram, tn, precision=high)
    gram = mapped_gram + lax.dot_general(
        jnp.concatenate([weight.T, crossed], axis=0),
        jnp.concatenate([crossed, weight.T], axis=0),
        tn,
        precision=high,
    )
    power_rows = lax.dynamic_slice_in_dim(mapped, row_start, rows_per, 0) + 0.05 * jnp.dot(
        grad_rows, crossed, precision=high
    )
    power_side = jnp.concatenate([mapped_back, mapped_grad], axis=1) + 0.05 * lax.dot_general(
        crossed, jnp.concatenate([grad_back, grad_gram], axis=1), tn, precision=high
    )
    right_new = 0.95 * right_factor + 0.05 * grad_gram
    right_power = jnp.dot(right_new, right_basis, precision=high)
    right_gram = lax.dot_general(right_power, right_power, tn, precision=high)
    solved, right_inverse = factor_solve(
        gram, jnp.concatenate([power_side, power_rows.T], axis=1), right_gram
    )
    turned_momentum = solved[:, :channels]
    turned_grad = solved[:, channels : 2 * channels]
    basis_new = solved[:, 2 * channels :].T
    right_basis_new = lax.dot_general(
        right_power, right_inverse, (((1,), (1,)), ((), ())), precision=high
    )
    right_turn = lax.dot_general(right_basis, right_basis_new, tn, precision=high)
    rotated = jnp.dot(turned_momentum, right_turn, precision=high)
    projected = jnp.dot(turned_grad, right_basis_new, precision=high)
    momentum_all = 0.9 * rotated + 0.1 * projected
    second_all = 0.95 * all_second + 0.05 * projected * projected
    normalized = momentum_all / (jnp.sqrt(second_all) + epsilon)
    momentum_new = lax.dynamic_slice_in_dim(momentum_all, moment_start, moment_rows, 0)
    second_new = lax.dynamic_slice_in_dim(second_all, moment_start, moment_rows, 0)
    update_rows = jnp.dot(basis_new, normalized, precision=high)
    update = lax.dot_general(
        update_rows, right_basis_new, (((1,), (1,)), ((), ())), precision=high
    )
    return (
        result,
        input_grad,
        grad,
        left_new,
        basis_new,
        right_new,
        right_basis_new,
        momentum_new,
        second_new,
        update,
    )


def solution(mesh):
    placed = (
        P(("group", "dp"), "tile", None, None, None),
        P(("group", "dp"), "tile", None, None, None),
        P("group", None),
        P("tile"),
        P("tile", None),
        P(("group", "tile"), None),
        P(("group", "tile"), "dp"),
        P("group", None),
        P("group", None),
        P(("group", "dp"), None),
        P(("group", "dp"), None),
    )
    return jax.shard_map(
        body,
        mesh=mesh,
        in_specs=placed,
        out_specs=(
            P(("group", "dp"), "tile", None, None, None),
            P(("group", "dp"), "tile", None, None, None),
            P("group", None),
            P(("group", "tile"), None),
            P(("group", "tile"), None),
            P("group", None),
            P("group", None),
            P(("group", "dp"), None),
            P(("group", "dp"), None),
            P(("group", "tile"), None),
        ),
        check_vma=False,
    )
```

```python
import math

import jax
import jax.numpy as jnp
from jax import lax
from jax.experimental import pallas as pl
from jax.experimental.pallas import tpu as pltpu
from jax.sharding import PartitionSpec as P

highest = lax.Precision.HIGHEST
epsilon = 1e-08


def edge_strips(values):
    return jnp.stack(
        [values[..., 0, :, :], values[..., :, -1, :], values[..., -1, :, :], values[..., :, 0, :]],
        axis=0,
    )


def cycle_strips(spread):
    return jnp.stack(
        [spread[:, 0, 1:-1], spread[:, 1:-1, -1], spread[:, -1, 1:-1], spread[:, 1:-1, 0]], axis=0
    )


def assemble(tile_vals, borders):
    middle = jnp.concatenate(
        [borders[3][:, :, None, :], tile_vals, borders[1][:, :, None, :]], axis=2
    )
    top_row = jnp.pad(borders[0], ((0, 0), (1, 1), (0, 0)))[:, None]
    bottom_row = jnp.pad(borders[2], ((0, 0), (1, 1), (0, 0)))[:, None]
    return jnp.concatenate([top_row, middle, bottom_row], axis=1)


def tap_patches(padded, side):
    pieces = [
        padded[:, row_off : row_off + side, col_off : col_off + side, :]
        for row_off in range(3)
        for col_off in range(3)
    ]
    joined = jnp.concatenate(pieces, axis=-1)
    return joined.reshape(-1, joined.shape[-1])


def spread_back(flat_grads, kernel, sample_count, side):
    channels = kernel.shape[1]
    summed = jnp.zeros((sample_count, side + 2, side + 2, channels), jnp.float32)
    for tap_index in range(9):
        row_off, col_off = divmod(tap_index, 3)
        weight_tap = kernel[tap_index * channels : (tap_index + 1) * channels]
        contrib = lax.dot_general(
            flat_grads, weight_tap, (((1,), (1,)), ((), ())), preferred_element_type=jnp.float32
        )
        contrib = contrib.reshape(sample_count, side, side, channels)
        summed = summed + jnp.pad(
            contrib, ((0, 0), (row_off, 2 - row_off), (col_off, 2 - col_off), (0, 0))
        )
    return summed


def absorb_rims(interior, incoming):
    result = interior.at[..., 0, :, :].add(incoming[0])
    result = result.at[..., :, -1, :].add(incoming[1])
    result = result.at[..., -1, :, :].add(incoming[2])
    return result.at[..., :, 0, :].add(incoming[3])


def flip_edges(strips, flipped):
    return jnp.where(flipped[:, None, None, None], strips[:, :, ::-1, :], strips)


def pick_gathered(everything, near_tiles, facing, flipped, usable):
    flat = everything.reshape(everything.shape[0] * 4, -1)
    wanted = jnp.where(usable, near_tiles * 4 + facing, -1)
    selector = (lax.broadcasted_iota(jnp.int32, (4, flat.shape[0]), 1) == wanted[:, None]).astype(
        jnp.bfloat16
    )
    picked = jnp.dot(selector, flat, preferred_element_type=jnp.float32).astype(jnp.bfloat16)
    return flip_edges(picked.reshape((4,) + everything.shape[2:]), flipped)


LEAF = 128
SPAN = 384


def split(value):
    high = value.astype(jnp.bfloat16)
    return high, (value - high.astype(jnp.float32)).astype(jnp.bfloat16)


def split_wide(value):
    high = lax.reduce_precision(value, 8, 7)
    return high.astype(jnp.bfloat16), (value - high).astype(jnp.bfloat16)


def dot3(left, right, dims=(((1,), (0,)), ((), ()))):
    def one(a, b):
        return lax.dot_general(a, b, dims, preferred_element_type=jnp.float32)

    return one(left[0], right[0]) + (one(left[0], right[1]) + one(left[1], right[0]))


by_rows = (((1,), (1,)), ((), ()))


def leaf_inverse(block, m_ref, s_ref):
    row = lax.broadcasted_iota(jnp.int32, (LEAF, LEAF), 0)
    col = lax.broadcasted_iota(jnp.int32, (LEAF, LEAF), 1)
    on_diag = row == col
    unit = jnp.where(on_diag, 1.0, 0.0)
    kept = jnp.where(on_diag, block, 0.0)
    across = lax.rsqrt(jnp.sum(kept, axis=0, keepdims=True))
    down = lax.rsqrt(jnp.sum(kept, axis=1, keepdims=True))
    scaled = block * across * down
    m_ref[...] = jnp.where(on_diag, down, jnp.where(row > col, -scaled * across, 0.0))
    pair = split(block)

    def more(carry):
        step, error = carry
        return (step < 12) & (error > 1e-4)

    def refine(carry):
        step, _ = carry
        guess = m_ref[...]
        guess_pair = split(guess)
        turned = dot3(guess_pair, pair)
        gap = dot3(split(turned), guess_pair, by_rows) - unit
        error = jnp.max(jnp.abs(gap))
        low = jnp.where(row > col, gap, jnp.where(on_diag, 0.5 * gap, 0.0))
        m_ref[...] = guess - dot3(split(low), guess_pair)
        return step + 1, error

    _, error = lax.while_loop(more, refine, (jnp.int32(0), jnp.float32(1.0)))

    @pl.when(jnp.logical_not(error <= 1e-4))
    def _():
        s_ref[...] = block
        m_ref[...] = unit

        def eliminate(j, carry):
            work = s_ref[...]
            line = s_ref[pl.ds(j, 1), :]
            lane = lax.broadcasted_iota(jnp.int32, (1, LEAF), 1)
            scale = lax.rsqrt(jnp.sum(jnp.where(lane == j, line, 0.0), axis=1, keepdims=True))
            column = jnp.sum(jnp.where(col == j, work, 0.0), axis=1, keepdims=True)
            side = lax.broadcasted_iota(jnp.int32, (LEAF, 1), 0)
            column = jnp.where(side > j, column * scale, 0.0)
            s_ref[...] = work - column * (line * scale)
            mine = m_ref[pl.ds(j, 1), :] * scale
            m_ref[...] = m_ref[...] - column * mine
            m_ref[pl.ds(j, 1), :] = mine
            return carry

        lax.fori_loop(0, LEAF, eliminate, 0)


def factor_kernel(
    gram_ref, side_ref, small_ref, y_ref, small_out_ref, a_ref, uh, ul, uth, utl, yh, yl, m_ref, s_ref
):
    width = gram_ref.shape[1]
    blocks = width // LEAF
    spans = width // SPAN
    leaf_inverse(small_ref[...], m_ref, s_ref)
    small_out_ref[...] = m_ref[...]
    a_ref[...] = gram_ref[...]
    y_ref[...] = side_ref[...]

    def block_step(k, carry):
        k0 = pl.multiple_of(k * LEAF, LEAF)
        leaf_inverse(a_ref[pl.ds(k0, LEAF), pl.ds(k0, LEAF)], m_ref, s_ref)
        inverse = split(m_ref[...])
        for span in range(spans):
            part = slice(span * SPAN, (span + 1) * SPAN)

            @pl.when((span + 1) * SPAN > k0 + LEAF)
            def _():
                value = dot3(inverse, split(a_ref[pl.ds(k0, LEAF), part]))
                uh[:, part], ul[:, part] = split(value)
                uth[part, :], utl[part, :] = split(value.T)

        value = dot3(inverse, split(y_ref[pl.ds(k0, LEAF), :]))
        y_ref[pl.ds(k0, LEAF), :] = value
        yh[...], yl[...] = split(value)

        def row_step(i, inner):
            i0 = pl.multiple_of(i * LEAF, LEAF)
            left = uth[pl.ds(i0, LEAF), :], utl[pl.ds(i0, LEAF), :]
            for span in range(spans):
                part = slice(span * SPAN, (span + 1) * SPAN)

                @pl.when((span + 1) * SPAN > i0)
                def _():
                    a_ref[pl.ds(i0, LEAF), part] -= dot3(left, (uh[:, part], ul[:, part]))

            y_ref[pl.ds(i0, LEAF), :] -= dot3(left, (yh[...], yl[...]))
            return inner

        lax.fori_loop(k + 1, blocks, row_step, 0)
        return carry

    lax.fori_loop(0, blocks, block_step, 0)


def factor_solve(gram, side, small):
    width, columns = side.shape
    vmem = pl.BlockSpec(memory_space=pltpu.VMEM)
    half = jnp.bfloat16
    return pl.pallas_call(
        factor_kernel,
        out_shape=(
            jax.ShapeDtypeStruct(side.shape, jnp.float32),
            jax.ShapeDtypeStruct(small.shape, jnp.float32),
        ),
        in_specs=[vmem] * 3,
        out_specs=(vmem, vmem),
        scratch_shapes=[
            pltpu.VMEM((width, width), jnp.float32),
            pltpu.VMEM((LEAF, width), half),
            pltpu.VMEM((LEAF, width), half),
            pltpu.VMEM((width, LEAF), half),
            pltpu.VMEM((width, LEAF), half),
            pltpu.VMEM((LEAF, columns), half),
            pltpu.VMEM((LEAF, columns), half),
            pltpu.VMEM((LEAF, LEAF), jnp.float32),
            pltpu.VMEM((LEAF, LEAF), jnp.float32),
        ],
        compiler_params=pltpu.CompilerParams(vmem_limit_bytes=40 * 1024 * 1024),
        name="factor_solve",
    )(gram, side, small)


high = lax.Precision.HIGH
tn = (((0,), (0,)), ((), ()))


def sum_kernel(dp_count, tiles, x_ref, out_ref, near, part, far, *sems):
    dp_index = lax.axis_index("dp")
    tile_index = lax.axis_index("tile")
    dp_peers = [lax.rem(dp_index + step, dp_count) for step in range(1, dp_count)]
    tile_peers = [lax.rem(tile_index + step, tiles) for step in range(1, tiles)]
    barrier = pltpu.get_barrier_semaphore()
    for axis, peers in (("dp", dp_peers), ("tile", tile_peers)):
        for peer in peers:
            pl.semaphore_signal(
                barrier, inc=1, device_id={axis: peer}, device_id_type=pl.DeviceIdType.MESH
            )
    pl.semaphore_wait(barrier, dp_count + tiles - 2)

    def exchange(axis, peers, source, target, send, receive):
        copies = [
            pltpu.make_async_remote_copy(
                src_ref=source(peer),
                dst_ref=target(slot),
                send_sem=send.at[slot],
                recv_sem=receive.at[slot],
                device_id={axis: peer},
                device_id_type=pl.DeviceIdType.MESH,
            )
            for slot, peer in enumerate(peers)
        ]
        for copy in copies:
            copy.start()
        for copy in copies:
            copy.wait()

    exchange("dp", dp_peers, lambda peer: x_ref.at[peer], lambda slot: near.at[slot], *sems[0:2])
    total = x_ref[dp_index]
    for slot in range(dp_count - 1):
        total = total + near[slot]
    part[...] = total
    exchange("tile", tile_peers, lambda peer: part.at[peer], lambda slot: far.at[slot], *sems[2:4])
    total = part[tile_index]
    for slot in range(tiles - 1):
        total = total + far[slot]
    out_ref[dp_index, tile_index] = total
    own = out_ref.at[dp_index, tile_index]
    exchange("tile", tile_peers, lambda peer: own, lambda slot: own, *sems[4:6])
    slab = out_ref.at[dp_index]
    exchange("dp", dp_peers, lambda peer: slab, lambda slot: slab, *sems[6:8])


def sum_everywhere(value):
    tiles = lax.axis_size("tile")
    dp_count = lax.axis_size("dp")
    rows, columns = value.shape
    if tiles < 2 or dp_count < 2 or rows % (tiles * dp_count):
        return lax.psum(value, ("tile", "dp"))
    piece = rows // (tiles * dp_count)
    vmem = pl.BlockSpec(memory_space=pltpu.VMEM)
    wide = (dp_count, tiles, piece, columns)
    counts = [dp_count - 1] * 2 + [tiles - 1] * 4 + [dp_count - 1] * 2
    out = pl.pallas_call(
        lambda *refs: sum_kernel(dp_count, tiles, *refs),
        out_shape=jax.ShapeDtypeStruct(wide, jnp.float32),
        in_specs=[vmem],
        out_specs=vmem,
        scratch_shapes=[
            pltpu.VMEM((dp_count - 1, tiles, piece, columns), jnp.float32),
            pltpu.VMEM((tiles, piece, columns), jnp.float32),
            pltpu.VMEM((tiles - 1, piece, columns), jnp.float32),
            *[pltpu.SemaphoreType.DMA((count,)) for count in counts],
        ],
        compiler_params=pltpu.CompilerParams(collective_id=0, has_side_effects=True),
        name="sum_everywhere",
    )(value.reshape(wide))
    return out.reshape(rows, columns)


def body(
    activations,
    cotangent,
    kernel,
    turning,
    orient,
    left_factor,
    left_basis,
    right_factor,
    right_basis,
    momentum,
    second_moment,
):
    tiles = lax.axis_size("tile")
    dp_count = lax.axis_size("dp")
    tile_index = lax.axis_index("tile")
    dp_index = lax.axis_index("dp")
    tile_vals = activations[:, 0]
    tile_grads = cotangent[:, 0]
    sample_count = tile_vals.shape[0]
    side = tile_vals.shape[1]
    channels = tile_vals.shape[-1]
    own_turn = turning[0]
    facing = orient[0] % 4
    flipped = orient[0] >= 4
    heading = (jnp.arange(4, dtype=jnp.int32) + own_turn) % 4
    row_of = tile_index // 4
    col_of = tile_index % 4
    room = jnp.stack([row_of > 0, col_of < 3, row_of < tiles // 4 - 1, col_of > 0])
    usable = (
        jnp.sum(
            jnp.where(
                heading[:, None] == jnp.arange(4, dtype=jnp.int32)[None, :], room[None, :], False
            ),
            axis=1,
        )
        > 0
    )
    offsets = jnp.array([-4, 1, 4, -1], dtype=jnp.int32)
    near_tiles = tile_index + jnp.sum(
        jnp.where(heading[:, None] == jnp.arange(4, dtype=jnp.int32)[None, :], offsets[None, :], 0),
        axis=1,
    )
    strips = edge_strips(tile_vals)
    flat_grads = tile_grads.reshape(-1, channels)
    spread = spread_back(flat_grads, kernel, sample_count, side)
    rim_cells = cycle_strips(spread).astype(jnp.bfloat16)
    everything = lax.all_gather(
        jnp.concatenate([strips, rim_cells], axis=0)[None], "tile", axis=0, tiled=True
    )
    borders = pick_gathered(everything[:, :4], near_tiles, facing, flipped, usable)
    incoming = pick_gathered(everything[:, 4:], near_tiles, facing, flipped, usable)
    padded = assemble(tile_vals, borders)
    columns = tap_patches(padded, side)
    partial_grad = lax.dot_general(
        columns, flat_grads, (((0,), (0,)), ((), ())), preferred_element_type=jnp.float32
    )
    summed_grad = sum_everywhere(partial_grad)
    result = jnp.dot(columns, kernel, preferred_element_type=jnp.float32).astype(jnp.bfloat16)
    result = result.reshape(activations.shape)
    input_grad = absorb_rims(spread[:, 1:-1, 1:-1], incoming.astype(jnp.float32)).astype(
        jnp.bfloat16
    )
    input_grad = input_grad.reshape(cotangent.shape)
    cells = dp_count * sample_count * tiles * side * side
    grad = summed_grad * (1.0 / math.sqrt(cells))
    rows_per, width = left_factor.shape
    row_start = tile_index * rows_per
    moment_rows = momentum.shape[0]
    moment_start = dp_index * moment_rows
    grad_rows = lax.dynamic_slice_in_dim(grad, row_start, rows_per, 0)
    left_new = 0.95 * left_factor + 0.05 * lax.dot_general(
        grad_rows, grad, (((1,), (1,)), ((), ())), precision=high
    )
    basis_rows = lax.all_gather(left_basis, "dp", axis=1, tiled=True)
    basis = lax.all_gather(basis_rows.astype(jnp.bfloat16), "tile", axis=0, tiled=True)
    moments = lax.all_gather(
        jnp.concatenate([momentum, second_moment], axis=1), "dp", axis=0, tiled=True
    )
    all_momentum, all_second = moments[:, :channels], moments[:, channels:]
    back_rows = jnp.dot(basis_rows, all_momentum, precision=highest)
    own_row = row_start + lax.broadcasted_iota(jnp.int32, left_factor.shape, 0)
    own_col = lax.broadcasted_iota(jnp.int32, left_factor.shape, 1)
    diagonal = jnp.sum(jnp.where(own_row == own_col, left_factor, 0.0), axis=1, keepdims=True)
    rest = jnp.broadcast_to(split_wide(diagonal)[1], (rows_per, LEAF))
    factor = lax.all_gather(
        jnp.concatenate(
            [left_factor.astype(jnp.bfloat16), *split_wide(back_rows), rest], axis=1
        ),
        "tile",
        axis=0,
        tiled=True,
    )
    back = factor[:, width : width + channels].astype(jnp.float32) + factor[
        :, width + channels : width + 2 * channels
    ].astype(jnp.float32)
    rest = factor[:, width + 2 * channels : width + 2 * channels + 1]
    factor = factor[:, :width]
    mapped = 0.95 * (
        jnp.dot(factor, basis, preferred_element_type=jnp.float32)
        + rest.astype(jnp.float32) * basis.astype(jnp.float32)
    )
    mapped_gram = lax.dot_general(mapped, mapped, tn, precision=high)
    mapped_back = lax.dot_general(mapped, back, tn, precision=high)
    crossed = sum(
        lax.dot_general(term, basis, tn, preferred_element_type=jnp.float32) for term in split_wide(grad)
    )
    mapped_grad = lax.dot_general(mapped, grad, tn, precision=high)
    grad_gram = lax.dot_general(grad, grad, tn, precision=high)
    grad_back = lax.dot_general(grad, back, tn, precision=high)
    weight = 0.05 * mapped_grad + 0.00125 * lax.dot_general(crossed, grad_gram, tn, precision=high)
    gram = mapped_gram + lax.dot_general(
        jnp.concatenate([weight.T, crossed], axis=0),
        jnp.concatenate([crossed, weight.T], axis=0),
        tn,
        precision=high,
    )
    power_rows = lax.dynamic_slice_in_dim(mapped, row_start, rows_per, 0) + 0.05 * jnp.dot(
        grad_rows, crossed, precision=high
    )
    power_side = jnp.concatenate([mapped_back, mapped_grad], axis=1) + 0.05 * lax.dot_general(
        crossed, jnp.concatenate([grad_back, grad_gram], axis=1), tn, precision=high
    )
    right_new = 0.95 * right_factor + 0.05 * grad_gram
    right_power = jnp.dot(right_new, right_basis, precision=high)
    right_gram = lax.dot_general(right_power, right_power, tn, precision=high)
    solved, right_inverse = factor_solve(
        gram, jnp.concatenate([power_side, power_rows.T], axis=1), right_gram
    )
    turned_momentum = solved[:, :channels]
    turned_grad = solved[:, channels : 2 * channels]
    basis_new = solved[:, 2 * channels :].T
    right_basis_new = lax.dot_general(
        right_power, right_inverse, (((1,), (1,)), ((), ())), precision=high
    )
    right_turn = lax.dot_general(right_basis, right_basis_new, tn, precision=high)
    rotated = jnp.dot(turned_momentum, right_turn, precision=high)
    projected = jnp.dot(turned_grad, right_basis_new, precision=high)
    momentum_all = 0.9 * rotated + 0.1 * projected
    second_all = 0.95 * all_second + 0.05 * projected * projected
    normalized = momentum_all / (jnp.sqrt(second_all) + epsilon)
    momentum_new = lax.dynamic_slice_in_dim(momentum_all, moment_start, moment_rows, 0)
    second_new = lax.dynamic_slice_in_dim(second_all, moment_start, moment_rows, 0)
    update_rows = jnp.dot(basis_new, normalized, precision=high)
    update = lax.dot_general(
        update_rows, right_basis_new, (((1,), (1,)), ((), ())), precision=high
    )
    return (
        result,
        input_grad,
        grad,
        left_new,
        basis_new,
        right_new,
        right_basis_new,
        momentum_new,
        second_new,
        update,
    )


def solution(mesh):
    placed = (
        P(("group", "dp"), "tile", None, None, None),
        P(("group", "dp"), "tile", None, None, None),
        P("group", None),
        P("tile"),
        P("tile", None),
        P(("group", "tile"), None),
        P(("group", "tile"), "dp"),
        P("group", None),
        P("group", None),
        P(("group", "dp"), None),
        P(("group", "dp"), None),
    )
    return jax.shard_map(
        body,
        mesh=mesh,
        in_specs=placed,
        out_specs=(
            P(("group", "dp"), "tile", None, None, None),
            P(("group", "dp"), "tile", None, None, None),
            P("group", None),
            P(("group", "tile"), None),
            P(("group", "tile"), None),
            P("group", None),
            P("group", None),
            P(("group", "dp"), None),
            P(("group", "dp"), None),
            P(("group", "tile"), None),
        ),
        check_vma=False,
    )
```

```python
import math

import jax
import jax.numpy as jnp
from jax import lax
from jax.experimental import pallas as pl
from jax.experimental.pallas import tpu as pltpu
from jax.sharding import PartitionSpec as P

highest = lax.Precision.HIGHEST
epsilon = 1e-08


def edge_strips(values):
    return jnp.stack(
        [values[..., 0, :, :], values[..., :, -1, :], values[..., -1, :, :], values[..., :, 0, :]],
        axis=0,
    )


def cycle_strips(spread):
    return jnp.stack(
        [spread[:, 0, 1:-1], spread[:, 1:-1, -1], spread[:, -1, 1:-1], spread[:, 1:-1, 0]], axis=0
    )


def assemble(tile_vals, borders):
    middle = jnp.concatenate(
        [borders[3][:, :, None, :], tile_vals, borders[1][:, :, None, :]], axis=2
    )
    top_row = jnp.pad(borders[0], ((0, 0), (1, 1), (0, 0)))[:, None]
    bottom_row = jnp.pad(borders[2], ((0, 0), (1, 1), (0, 0)))[:, None]
    return jnp.concatenate([top_row, middle, bottom_row], axis=1)


def tap_patches(padded, side):
    pieces = [
        padded[:, row_off : row_off + side, col_off : col_off + side, :]
        for row_off in range(3)
        for col_off in range(3)
    ]
    joined = jnp.concatenate(pieces, axis=-1)
    return joined.reshape(-1, joined.shape[-1])


def spread_back(flat_grads, kernel, sample_count, side):
    channels = kernel.shape[1]
    summed = jnp.zeros((sample_count, side + 2, side + 2, channels), jnp.float32)
    for tap_index in range(9):
        row_off, col_off = divmod(tap_index, 3)
        weight_tap = kernel[tap_index * channels : (tap_index + 1) * channels]
        contrib = lax.dot_general(
            flat_grads, weight_tap, (((1,), (1,)), ((), ())), preferred_element_type=jnp.float32
        )
        contrib = contrib.reshape(sample_count, side, side, channels)
        summed = summed + jnp.pad(
            contrib, ((0, 0), (row_off, 2 - row_off), (col_off, 2 - col_off), (0, 0))
        )
    return summed


def absorb_rims(interior, incoming):
    result = interior.at[..., 0, :, :].add(incoming[0])
    result = result.at[..., :, -1, :].add(incoming[1])
    result = result.at[..., -1, :, :].add(incoming[2])
    return result.at[..., :, 0, :].add(incoming[3])


def flip_edges(strips, flipped):
    return jnp.where(flipped[:, None, None, None], strips[:, :, ::-1, :], strips)


def pick_gathered(everything, near_tiles, facing, flipped, usable):
    flat = everything.reshape(everything.shape[0] * 4, -1)
    wanted = jnp.where(usable, near_tiles * 4 + facing, -1)
    selector = (lax.broadcasted_iota(jnp.int32, (4, flat.shape[0]), 1) == wanted[:, None]).astype(
        jnp.bfloat16
    )
    picked = jnp.dot(selector, flat, preferred_element_type=jnp.float32).astype(jnp.bfloat16)
    return flip_edges(picked.reshape((4,) + everything.shape[2:]), flipped)


LEAF = 128
SPAN = 384


def split(value):
    high = value.astype(jnp.bfloat16)
    return high, (value - high.astype(jnp.float32)).astype(jnp.bfloat16)


def split_wide(value):
    high = lax.reduce_precision(value, 8, 7)
    return high.astype(jnp.bfloat16), (value - high).astype(jnp.bfloat16)


def dot3(left, right, dims=(((1,), (0,)), ((), ()))):
    def one(a, b):
        return lax.dot_general(a, b, dims, preferred_element_type=jnp.float32)

    return one(left[0], right[0]) + (one(left[0], right[1]) + one(left[1], right[0]))


by_rows = (((1,), (1,)), ((), ()))


def leaf_inverse(block, m_ref, s_ref):
    row = lax.broadcasted_iota(jnp.int32, (LEAF, LEAF), 0)
    col = lax.broadcasted_iota(jnp.int32, (LEAF, LEAF), 1)
    on_diag = row == col
    unit = jnp.where(on_diag, 1.0, 0.0)
    kept = jnp.where(on_diag, block, 0.0)
    across = lax.rsqrt(jnp.sum(kept, axis=0, keepdims=True))
    down = lax.rsqrt(jnp.sum(kept, axis=1, keepdims=True))
    scaled = block * across * down
    m_ref[...] = jnp.where(on_diag, down, jnp.where(row > col, -scaled * across, 0.0))
    pair = split(block)
    rough = m_ref[...].astype(jnp.bfloat16)
    turned = jnp.dot(rough, pair[0], preferred_element_type=jnp.float32).astype(jnp.bfloat16)
    gap = lax.dot_general(turned, rough, by_rows, preferred_element_type=jnp.float32) - unit
    low = jnp.where(row > col, gap, jnp.where(on_diag, 0.5 * gap, 0.0)).astype(jnp.bfloat16)
    m_ref[...] -= jnp.dot(low, rough, preferred_element_type=jnp.float32)

    def more(carry):
        step, error = carry
        return (step < 12) & (error > 1e-4)

    def refine(carry):
        step, _ = carry
        guess = m_ref[...]
        guess_pair = split(guess)
        turned = dot3(guess_pair, pair)
        gap = dot3(split(turned), guess_pair, by_rows) - unit
        error = jnp.max(jnp.abs(gap))
        low = jnp.where(row > col, gap, jnp.where(on_diag, 0.5 * gap, 0.0))
        m_ref[...] = guess - dot3(split(low), guess_pair)
        return step + 1, error

    _, error = lax.while_loop(more, refine, (jnp.int32(0), jnp.float32(1.0)))

    @pl.when(jnp.logical_not(error <= 1e-4))
    def _():
        s_ref[...] = block
        m_ref[...] = unit

        def eliminate(j, carry):
            work = s_ref[...]
            line = s_ref[pl.ds(j, 1), :]
            lane = lax.broadcasted_iota(jnp.int32, (1, LEAF), 1)
            scale = lax.rsqrt(jnp.sum(jnp.where(lane == j, line, 0.0), axis=1, keepdims=True))
            column = jnp.sum(jnp.where(col == j, work, 0.0), axis=1, keepdims=True)
            side = lax.broadcasted_iota(jnp.int32, (LEAF, 1), 0)
            column = jnp.where(side > j, column * scale, 0.0)
            s_ref[...] = work - column * (line * scale)
            mine = m_ref[pl.ds(j, 1), :] * scale
            m_ref[...] = m_ref[...] - column * mine
            m_ref[pl.ds(j, 1), :] = mine
            return carry

        lax.fori_loop(0, LEAF, eliminate, 0)


def factor_kernel(
    gram_ref, side_ref, small_ref, y_ref, small_out_ref, a_ref, uh, ul, uth, utl, yh, yl, m_ref, s_ref
):
    width = gram_ref.shape[1]
    blocks = width // LEAF
    spans = width // SPAN
    leaf_inverse(small_ref[...], m_ref, s_ref)
    small_out_ref[...] = m_ref[...]
    a_ref[...] = gram_ref[...]
    y_ref[...] = side_ref[...]

    def block_step(k, carry):
        k0 = pl.multiple_of(k * LEAF, LEAF)
        leaf_inverse(a_ref[pl.ds(k0, LEAF), pl.ds(k0, LEAF)], m_ref, s_ref)
        inverse = split(m_ref[...])
        for span in range(spans):
            part = slice(span * SPAN, (span + 1) * SPAN)

            @pl.when((span + 1) * SPAN > k0 + LEAF)
            def _():
                value = dot3(inverse, split(a_ref[pl.ds(k0, LEAF), part]))
                uh[:, part], ul[:, part] = split(value)
                uth[part, :], utl[part, :] = split(value.T)

        value = dot3(inverse, split(y_ref[pl.ds(k0, LEAF), :]))
        y_ref[pl.ds(k0, LEAF), :] = value
        yh[...], yl[...] = split(value)

        def row_step(i, inner):
            i0 = pl.multiple_of(i * LEAF, LEAF)
            left = uth[pl.ds(i0, LEAF), :], utl[pl.ds(i0, LEAF), :]
            for span in range(spans):
                part = slice(span * SPAN, (span + 1) * SPAN)

                @pl.when((span + 1) * SPAN > i0)
                def _():
                    a_ref[pl.ds(i0, LEAF), part] -= dot3(left, (uh[:, part], ul[:, part]))

            y_ref[pl.ds(i0, LEAF), :] -= dot3(left, (yh[...], yl[...]))
            return inner

        lax.fori_loop(k + 1, blocks, row_step, 0)
        return carry

    lax.fori_loop(0, blocks, block_step, 0)


def factor_solve(gram, side, small):
    width, columns = side.shape
    vmem = pl.BlockSpec(memory_space=pltpu.VMEM)
    half = jnp.bfloat16
    return pl.pallas_call(
        factor_kernel,
        out_shape=(
            jax.ShapeDtypeStruct(side.shape, jnp.float32),
            jax.ShapeDtypeStruct(small.shape, jnp.float32),
        ),
        in_specs=[vmem] * 3,
        out_specs=(vmem, vmem),
        scratch_shapes=[
            pltpu.VMEM((width, width), jnp.float32),
            pltpu.VMEM((LEAF, width), half),
            pltpu.VMEM((LEAF, width), half),
            pltpu.VMEM((width, LEAF), half),
            pltpu.VMEM((width, LEAF), half),
            pltpu.VMEM((LEAF, columns), half),
            pltpu.VMEM((LEAF, columns), half),
            pltpu.VMEM((LEAF, LEAF), jnp.float32),
            pltpu.VMEM((LEAF, LEAF), jnp.float32),
        ],
        compiler_params=pltpu.CompilerParams(vmem_limit_bytes=40 * 1024 * 1024),
        name="factor_solve",
    )(gram, side, small)


high = lax.Precision.HIGH
tn = (((0,), (0,)), ((), ()))


def sum_kernel(dp_count, tiles, x_ref, out_ref, near, part, far, *sems):
    dp_index = lax.axis_index("dp")
    tile_index = lax.axis_index("tile")
    dp_peers = [lax.rem(dp_index + step, dp_count) for step in range(1, dp_count)]
    tile_peers = [lax.rem(tile_index + step, tiles) for step in range(1, tiles)]
    barrier = pltpu.get_barrier_semaphore()
    for axis, peers in (("dp", dp_peers), ("tile", tile_peers)):
        for peer in peers:
            pl.semaphore_signal(
                barrier, inc=1, device_id={axis: peer}, device_id_type=pl.DeviceIdType.MESH
            )
    pl.semaphore_wait(barrier, dp_count + tiles - 2)

    def exchange(axis, peers, source, target, send, receive):
        copies = [
            pltpu.make_async_remote_copy(
                src_ref=source(peer),
                dst_ref=target(slot),
                send_sem=send.at[slot],
                recv_sem=receive.at[slot],
                device_id={axis: peer},
                device_id_type=pl.DeviceIdType.MESH,
            )
            for slot, peer in enumerate(peers)
        ]
        for copy in copies:
            copy.start()
        for copy in copies:
            copy.wait()

    exchange("dp", dp_peers, lambda peer: x_ref.at[peer], lambda slot: near.at[slot], *sems[0:2])
    total = x_ref[dp_index]
    for slot in range(dp_count - 1):
        total = total + near[slot]
    part[...] = total
    exchange("tile", tile_peers, lambda peer: part.at[peer], lambda slot: far.at[slot], *sems[2:4])
    total = part[tile_index]
    for slot in range(tiles - 1):
        total = total + far[slot]
    out_ref[dp_index, tile_index] = total
    own = out_ref.at[dp_index, tile_index]
    exchange("tile", tile_peers, lambda peer: own, lambda slot: own, *sems[4:6])
    slab = out_ref.at[dp_index]
    exchange("dp", dp_peers, lambda peer: slab, lambda slot: slab, *sems[6:8])


def sum_everywhere(value):
    tiles = lax.axis_size("tile")
    dp_count = lax.axis_size("dp")
    rows, columns = value.shape
    if tiles < 2 or dp_count < 2 or rows % (tiles * dp_count):
        return lax.psum(value, ("tile", "dp"))
    piece = rows // (tiles * dp_count)
    vmem = pl.BlockSpec(memory_space=pltpu.VMEM)
    wide = (dp_count, tiles, piece, columns)
    counts = [dp_count - 1] * 2 + [tiles - 1] * 4 + [dp_count - 1] * 2
    out = pl.pallas_call(
        lambda *refs: sum_kernel(dp_count, tiles, *refs),
        out_shape=jax.ShapeDtypeStruct(wide, jnp.float32),
        in_specs=[vmem],
        out_specs=vmem,
        scratch_shapes=[
            pltpu.VMEM((dp_count - 1, tiles, piece, columns), jnp.float32),
            pltpu.VMEM((tiles, piece, columns), jnp.float32),
            pltpu.VMEM((tiles - 1, piece, columns), jnp.float32),
            *[pltpu.SemaphoreType.DMA((count,)) for count in counts],
        ],
        compiler_params=pltpu.CompilerParams(collective_id=0, has_side_effects=True),
        name="sum_everywhere",
    )(value.reshape(wide))
    return out.reshape(rows, columns)


def body(
    activations,
    cotangent,
    kernel,
    turning,
    orient,
    left_factor,
    left_basis,
    right_factor,
    right_basis,
    momentum,
    second_moment,
):
    tiles = lax.axis_size("tile")
    dp_count = lax.axis_size("dp")
    tile_index = lax.axis_index("tile")
    dp_index = lax.axis_index("dp")
    tile_vals = activations[:, 0]
    tile_grads = cotangent[:, 0]
    sample_count = tile_vals.shape[0]
    side = tile_vals.shape[1]
    channels = tile_vals.shape[-1]
    own_turn = turning[0]
    facing = orient[0] % 4
    flipped = orient[0] >= 4
    heading = (jnp.arange(4, dtype=jnp.int32) + own_turn) % 4
    row_of = tile_index // 4
    col_of = tile_index % 4
    room = jnp.stack([row_of > 0, col_of < 3, row_of < tiles // 4 - 1, col_of > 0])
    usable = (
        jnp.sum(
            jnp.where(
                heading[:, None] == jnp.arange(4, dtype=jnp.int32)[None, :], room[None, :], False
            ),
            axis=1,
        )
        > 0
    )
    offsets = jnp.array([-4, 1, 4, -1], dtype=jnp.int32)
    near_tiles = tile_index + jnp.sum(
        jnp.where(heading[:, None] == jnp.arange(4, dtype=jnp.int32)[None, :], offsets[None, :], 0),
        axis=1,
    )
    strips = edge_strips(tile_vals)
    flat_grads = tile_grads.reshape(-1, channels)
    spread = spread_back(flat_grads, kernel, sample_count, side)
    rim_cells = cycle_strips(spread).astype(jnp.bfloat16)
    everything = lax.all_gather(
        jnp.concatenate([strips, rim_cells], axis=0)[None], "tile", axis=0, tiled=True
    )
    borders = pick_gathered(everything[:, :4], near_tiles, facing, flipped, usable)
    incoming = pick_gathered(everything[:, 4:], near_tiles, facing, flipped, usable)
    padded = assemble(tile_vals, borders)
    columns = tap_patches(padded, side)
    partial_grad = lax.dot_general(
        columns, flat_grads, (((0,), (0,)), ((), ())), preferred_element_type=jnp.float32
    )
    summed_grad = sum_everywhere(partial_grad)
    result = jnp.dot(columns, kernel, preferred_element_type=jnp.float32).astype(jnp.bfloat16)
    result = result.reshape(activations.shape)
    input_grad = absorb_rims(spread[:, 1:-1, 1:-1], incoming.astype(jnp.float32)).astype(
        jnp.bfloat16
    )
    input_grad = input_grad.reshape(cotangent.shape)
    cells = dp_count * sample_count * tiles * side * side
    grad = summed_grad * (1.0 / math.sqrt(cells))
    rows_per, width = left_factor.shape
    row_start = tile_index * rows_per
    moment_rows = momentum.shape[0]
    moment_start = dp_index * moment_rows
    grad_rows = lax.dynamic_slice_in_dim(grad, row_start, rows_per, 0)
    left_new = 0.95 * left_factor + 0.05 * lax.dot_general(
        grad_rows, grad, (((1,), (1,)), ((), ())), precision=high
    )
    basis_rows = lax.all_gather(left_basis, "dp", axis=1, tiled=True)
    basis = lax.all_gather(basis_rows.astype(jnp.bfloat16), "tile", axis=0, tiled=True)
    moments = lax.all_gather(
        jnp.concatenate([momentum, second_moment], axis=1), "dp", axis=0, tiled=True
    )
    all_momentum, all_second = moments[:, :channels], moments[:, channels:]
    back_rows = jnp.dot(basis_rows, all_momentum, precision=highest)
    own_row = row_start + lax.broadcasted_iota(jnp.int32, left_factor.shape, 0)
    own_col = lax.broadcasted_iota(jnp.int32, left_factor.shape, 1)
    diagonal = jnp.sum(jnp.where(own_row == own_col, left_factor, 0.0), axis=1, keepdims=True)
    rest = jnp.broadcast_to(split_wide(diagonal)[1], (rows_per, LEAF))
    factor = lax.all_gather(
        jnp.concatenate(
            [left_factor.astype(jnp.bfloat16), *split_wide(back_rows), rest], axis=1
        ),
        "tile",
        axis=0,
        tiled=True,
    )
    back = factor[:, width : width + channels].astype(jnp.float32) + factor[
        :, width + channels : width + 2 * channels
    ].astype(jnp.float32)
    rest = factor[:, width + 2 * channels : width + 2 * channels + 1]
    factor = factor[:, :width]
    mapped = 0.95 * (
        jnp.dot(factor, basis, preferred_element_type=jnp.float32)
        + rest.astype(jnp.float32) * basis.astype(jnp.float32)
    )
    mapped_gram = lax.dot_general(mapped, mapped, tn, precision=high)
    mapped_back = lax.dot_general(mapped, back, tn, precision=high)
    crossed = sum(
        lax.dot_general(term, basis, tn, preferred_element_type=jnp.float32) for term in split_wide(grad)
    )
    mapped_grad = lax.dot_general(mapped, grad, tn, precision=high)
    grad_gram = lax.dot_general(grad, grad, tn, precision=high)
    grad_back = lax.dot_general(grad, back, tn, precision=high)
    weight = 0.05 * mapped_grad + 0.00125 * lax.dot_general(crossed, grad_gram, tn, precision=high)
    gram = mapped_gram + lax.dot_general(
        jnp.concatenate([weight.T, crossed], axis=0),
        jnp.concatenate([crossed, weight.T], axis=0),
        tn,
        precision=high,
    )
    power_rows = lax.dynamic_slice_in_dim(mapped, row_start, rows_per, 0) + 0.05 * jnp.dot(
        grad_rows, crossed, precision=high
    )
    power_side = jnp.concatenate([mapped_back, mapped_grad], axis=1) + 0.05 * lax.dot_general(
        crossed, jnp.concatenate([grad_back, grad_gram], axis=1), tn, precision=high
    )
    right_new = 0.95 * right_factor + 0.05 * grad_gram
    right_power = jnp.dot(right_new, right_basis, precision=high)
    right_gram = lax.dot_general(right_power, right_power, tn, precision=high)
    solved, right_inverse = factor_solve(
        gram, jnp.concatenate([power_side, power_rows.T], axis=1), right_gram
    )
    turned_momentum = solved[:, :channels]
    turned_grad = solved[:, channels : 2 * channels]
    basis_new = solved[:, 2 * channels :].T
    right_basis_new = lax.dot_general(
        right_power, right_inverse, (((1,), (1,)), ((), ())), precision=high
    )
    right_turn = lax.dot_general(right_basis, right_basis_new, tn, precision=high)
    rotated = jnp.dot(turned_momentum, right_turn, precision=high)
    projected = jnp.dot(turned_grad, right_basis_new, precision=high)
    momentum_all = 0.9 * rotated + 0.1 * projected
    second_all = 0.95 * all_second + 0.05 * projected * projected
    normalized = momentum_all / (jnp.sqrt(second_all) + epsilon)
    momentum_new = lax.dynamic_slice_in_dim(momentum_all, moment_start, moment_rows, 0)
    second_new = lax.dynamic_slice_in_dim(second_all, moment_start, moment_rows, 0)
    update_rows = jnp.dot(basis_new, normalized, precision=high)
    update = lax.dot_general(
        update_rows, right_basis_new, (((1,), (1,)), ((), ())), precision=high
    )
    return (
        result,
        input_grad,
        grad,
        left_new,
        basis_new,
        right_new,
        right_basis_new,
        momentum_new,
        second_new,
        update,
    )


def solution(mesh):
    placed = (
        P(("group", "dp"), "tile", None, None, None),
        P(("group", "dp"), "tile", None, None, None),
        P("group", None),
        P("tile"),
        P("tile", None),
        P(("group", "tile"), None),
        P(("group", "tile"), "dp"),
        P("group", None),
        P("group", None),
        P(("group", "dp"), None),
        P(("group", "dp"), None),
    )
    return jax.shard_map(
        body,
        mesh=mesh,
        in_specs=placed,
        out_specs=(
            P(("group", "dp"), "tile", None, None, None),
            P(("group", "dp"), "tile", None, None, None),
            P("group", None),
            P(("group", "tile"), None),
            P(("group", "tile"), None),
            P("group", None),
            P("group", None),
            P(("group", "dp"), None),
            P(("group", "dp"), None),
            P(("group", "tile"), None),
        ),
        check_vma=False,
    )
```
